256 devices in a mesh: cal: 64 (over z, y, core), gr: 4 (over x).
Axes of the slice: x: 4, y: 4, z: 8, core: 2. Of those that a mesh axis runs over, the one named last changes fastest.
Arguments:
- features: bfloat16 [131072, 4096], P('cal', 'gr'), may hold values from -6 to 6
- coef: bfloat16 [4096], P('gr'), may hold values from -0.09375 to 0.09375
- log_exposure: float32 [131072], P('cal'), may hold values from -0.7 to 0.7
- claims: float32 [131072], P('cal'), may hold values from 0 to 4
- cluster_id: int32 [131072], P('cal'), may hold values from 0 to 1023
- period: int32 [131072], P('cal'), may hold values from 0 to 127, as said below
- period_effect: float32 [128], replicated, may hold values from -0.5 to 0.5
Outputs:
- meat: float32 [4096, 4096], P('cal', 'gr')
The draws below stay inside these ranges and needn't reach their ends.
Inputs may be any that keep to these rules, and one draw needn't show every extreme that they name: `period`: rows of index d of cal lie in periods d * 2 to (d + 1) * 2 - 1.
All inputs are finite; a program needn't handle non-finite values.
Results may differ from the reference program's by a relative error of at most 0.0044.
Values sent between devices are 32-bit elements; how exact they have to be, the bound alone decides.
A program may use at most 64 MiB of HBM per device.

```python
import math
import jax
import jax.numpy as jnp
import numpy as np
from jax import lax

P_SIZE = 4096
ROWS_DEV = 2048
PER_DEV = 2
ROWS = 131072
CLUSTERS = 1024
PERIODS = 128


def draw_period(key, part):
    base = jnp.arange(ROWS, dtype=jnp.int32) // ROWS_DEV * PER_DEV
    extra = jax.random.randint(key, (ROWS,), 0, PER_DEV, dtype=jnp.int32)
    return (base + extra).astype(jnp.int32)


def touch_ends(entries, own_key, least, largest):
    longest = entries.shape.index(max(entries.shape))
    spots = []
    for shift in (0, 1):
        where = [jax.random.randint(jax.random.fold_in(own_key, axis), (), 0, length) for axis, length in enumerate(entries.shape)]
        where[longest] = (where[longest] + shift) % entries.shape[longest]
        spots.append(tuple(where))
    return entries.at[spots[0]].set(least).at[spots[1]].set(largest)


def levels(key, shape, pieces, least, high):
    def one(dim, blocks):
        steps = jax.random.uniform(jax.random.fold_in(jax.random.fold_in(key, 6), dim), (blocks,), jnp.float32, least / len(pieces), high / len(pieces))
        return jnp.repeat(jnp.exp(steps), shape[dim] // blocks).reshape((-1,) + (1,) * (len(shape) - dim - 1))

    loudness = one(*pieces[0])
    for cut in pieces[1:]:
        loudness = loudness * one(*cut)
    return loudness


def rank_bounds(amount, slope):
    loads = [(1 << 20) // math.isqrt(standing ** slope) + 1 for standing in range(1, amount + 1)]
    spread = 1 + sum(loads) // (1 << 30)
    return np.cumsum(np.array([max(1, weight // spread) for weight in loads]))


def skewed_ids(stream_key, extent, amount, skew):
    grid = rank_bounds(amount, skew)
    ticket = jax.random.randint(jax.random.fold_in(stream_key, 1), extent, 0, int(grid[amount - 1]))
    rank = jnp.searchsorted(jnp.asarray(grid, jnp.int32), ticket, side="right")
    return jax.random.permutation(jax.random.fold_in(stream_key, 2), amount)[rank].astype(jnp.int32)


def normal_values(own_key, shape, spread, limit, pieces=(), held_as=jnp.bfloat16):
    values = spread * jax.random.normal(own_key, shape, jnp.float32)
    if pieces:
        values = values * levels(own_key, shape, pieces, -0.22, 0.18)
    return jnp.clip(values, -limit, limit).astype(held_as)


def setup_inputs(seed: int = 0) -> dict:
    key_of = jax.random.split(jax.random.key(seed), 8)
    features = normal_values(key_of[0], (ROWS, P_SIZE), 1.0, 6.0, ((0, 64), (1, 4)))
    coef = normal_values(key_of[1], (P_SIZE,), P_SIZE ** -0.5, 0.09375, ((0, 4),))
    log_exposure = jnp.clip(jax.random.uniform(key_of[2], (ROWS,), jnp.float32, -0.7, 0.7) * levels(key_of[2], (ROWS,), ((0, 64),), -0.4, 0.0), -0.7, 0.7)
    claims = jnp.clip(4.0 * jax.random.uniform(key_of[3], (ROWS,), jnp.float32) ** levels(key_of[3], (ROWS,), ((0, 64),), -0.2, 0.2), 0.0, 4.0)
    cluster_id = touch_ends(skewed_ids(key_of[4], (ROWS,), CLUSTERS, 1), jax.random.fold_in(key_of[4], 3), 0, CLUSTERS - 1).astype(jnp.int32)
    period = draw_period(jax.random.fold_in(key_of[7], 71), 0)
    period_effect = jnp.clip(jax.random.uniform(key_of[6], (PERIODS,), jnp.float32, -0.5, 0.5), -0.5, 0.5)
    return dict(features=features, coef=coef, log_exposure=log_exposure, claims=claims, cluster_id=cluster_id, period=period, period_effect=period_effect)


def reference(features, coef, log_exposure, claims, cluster_id, period, period_effect):
    linear = jnp.dot(features, coef, preferred_element_type=jnp.float32)
    table = jnp.where(period[:, None] == jnp.arange(PERIODS, dtype=jnp.int32)[None, :], period_effect[None, :], jnp.float32(0.0))
    shift = jnp.sum(table, axis=1)
    resid = (claims - jnp.exp(linear + log_exposure + shift)).astype(jnp.bfloat16)
    block = ROWS_DEV
    count = ROWS // block
    feats = features.reshape(count, block, P_SIZE)
    res_b = resid.reshape(count, block)
    ids_b = cluster_id.reshape(count, block)

    def step(carry, item):
        feat_blk, res_blk, id_blk = item
        weighted = feat_blk.astype(jnp.float32) * res_blk.astype(jnp.float32)[:, None]
        return carry + jax.ops.segment_sum(weighted, id_blk, num_segments=CLUSTERS), None

    score, _ = lax.scan(step, jnp.zeros((CLUSTERS, P_SIZE), jnp.float32), (feats, res_b, ids_b))
    meat = jnp.dot(score.T, score, precision=lax.Precision.HIGHEST, preferred_element_type=jnp.float32)
    return meat / jnp.float32(ROWS)
```

```python
import functools
import jax
import jax.numpy as jnp
from jax import lax
from jax.experimental import pallas as pl
from jax.experimental.pallas import tpu as pltpu
from jax.sharding import PartitionSpec as P

MESH = pl.DeviceIdType.MESH
LANES = 128
NY = 4
SLICES = 2


def meat_kernel(
    nz, ny, nx,
    feat_hbm, coef_ref, logexp_ref, claims_ref, ids_ref, period_ref, eff_ref,
    out_ref,
    fbuf, lin, onehot, acc, give, take, rb1, rb2, full, lhs, part, part_in,
    load_sem, lin_ssem, lin_rsem, d2d_ssem, d2d_rsem,
    ring_ssem, ring_rsem, lhs_ssem, lhs_rsem, part_ssem, part_rsem,
):
    rows, width = feat_hbm.shape
    half = acc.shape[1]
    nchunk = acc.shape[0]
    tiles = fbuf.shape[0]
    tile_w = fbuf.shape[2]
    per_tile = tile_w // LANES
    span = half // SLICES
    cal = lax.axis_index("cal")
    x = lax.axis_index("gr")
    core = lax.rem(cal, 2)
    y = lax.rem(cal // 2, ny)
    z = cal // (2 * ny)

    def dev(z_, y_, core_, x_):
        return ((z_ * ny + y_) * 2 + core_, x_)

    def z_at(k):
        return dev(lax.rem(z + k + nz, nz), y, core, x)

    def y_at(k):
        return dev(z, lax.rem(y + k + ny, ny), core, x)

    partner = dev(z, y, 1 - core, x)

    def x_at(k):
        return (cal, lax.rem(x + k, nx))

    barrier = pltpu.get_barrier_semaphore()
    greet = [partner, z_at(1), z_at(-1), y_at(1), y_at(-1)] + [x_at(k) for k in range(1, nx)]
    for other in greet:
        pl.semaphore_signal(barrier, inc=1, device_id=other, device_id_type=MESH)

    def load(t):
        return pltpu.make_async_copy(
            feat_hbm.at[:, pl.ds(t * tile_w, tile_w)], fbuf.at[t], load_sem.at[t]
        )

    for t in range(tiles):
        load(t).start()
    total = None
    for t in range(tiles):
        load(t).wait()
        weights = jnp.broadcast_to(coef_ref[:, t * tile_w : (t + 1) * tile_w], (16, tile_w))
        term = lax.dot_general(
            weights, fbuf[t], (((1,), (1,)), ((), ())), preferred_element_type=jnp.float32
        )
        total = term if total is None else total + term
    lin[x] = total[0:1, :]

    pl.semaphore_wait(barrier, len(greet))

    def lin_copy(k):
        return pltpu.make_async_remote_copy(
            src_ref=lin.at[x], dst_ref=lin.at[x],
            send_sem=lin_ssem.at[k - 1], recv_sem=lin_rsem.at[k - 1],
            device_id=x_at(k), device_id_type=MESH,
        )

    def lin_arrival(k):
        origin = lax.rem(x - k + nx, nx)
        return pltpu.make_async_remote_copy(
            src_ref=lin.at[origin], dst_ref=lin.at[origin],
            send_sem=lin_ssem.at[k - 1], recv_sem=lin_rsem.at[k - 1],
            device_id=x_at(k), device_id_type=MESH,
        )

    for k in range(1, nx):
        lin_copy(k).start()
    first = cal * 2
    spots = lax.broadcasted_iota(jnp.int32, eff_ref.shape, 1)
    low = jnp.sum(jnp.where(spots == first, eff_ref[...], 0.0), axis=1, keepdims=True)
    high = jnp.sum(jnp.where(spots == first + 1, eff_ref[...], 0.0), axis=1, keepdims=True)
    shift = jnp.where(
        period_ref[...] == first, low, jnp.where(period_ref[...] == first + 1, high, 0.0)
    )
    for k in range(1, nx):
        lin_arrival(k).wait_recv()
    linear = lin[0]
    for k in range(1, nx):
        linear = linear + lin[k]
    resid = (claims_ref[...] - jnp.exp(linear + logexp_ref[...] + shift)).astype(jnp.bfloat16)
    resid = resid.astype(jnp.float32)
    ids = ids_ref[...]
    block = 64

    def pick(b, carry):
        base = pl.multiple_of(b * block, block)
        names = base + lax.broadcasted_iota(jnp.int32, (block, rows), 0)
        onehot[pl.ds(base, block), :] = jnp.where(names == ids, resid, 0.0).astype(jnp.bfloat16)
        return carry

    lax.fori_loop(0, 2 * half // block, pick, 0)

    per_z = nz // tiles
    per_y = ny // tiles if ny >= tiles else 1

    def anchor(which):
        return jnp.where(which == 0, z // per_z, y // per_y)

    def scores(which, t):
        picked = onehot[pl.ds(pl.multiple_of(which * half, half), half), :]
        return jnp.dot(picked, fbuf[t], preferred_element_type=jnp.float32)

    order = (2, 1, 3, 0)

    def swap(i, t):
        return pltpu.make_async_remote_copy(
            src_ref=give.at[pl.ds(t * per_tile, per_tile)],
            dst_ref=take.at[pl.ds(t * per_tile, per_tile)],
            send_sem=d2d_ssem.at[i], recv_sem=d2d_rsem.at[i],
            device_id=partner, device_id_type=MESH,
        )

    def theirs(i):
        return lax.rem(anchor(1 - core) + order[i], tiles)

    def mine(i):
        return lax.rem(anchor(core) + order[i], tiles)

    for i in range(tiles):
        t = theirs(i)
        res = scores(1 - core, t)
        for q in range(per_tile):
            give[t * per_tile + q] = res[:, q * LANES : (q + 1) * LANES]
        swap(i, t).start()

    def own_tile(i):
        t = mine(i)
        res = scores(core, t)
        swap(i, t).wait_recv()
        for q in range(per_tile):
            c = t * per_tile + q
            acc[c] = res[:, q * LANES : (q + 1) * LANES] + take[c]

    class Plan:
        def __init__(self, n1, n2, p1, p2, at1, at2):
            self.n = (n1, n2)
            self.p = (p1, p2)
            self.at = (at1, at2)
            self.w = nchunk // n1
            self.piece = span // n2

        def hops(self, axis, u, d):
            n = self.n[axis]
            return n // 2 if u % 2 == d else n // 2 - 1

        def chunk(self, ref, axis, u, owner):
            if axis == 0:
                return ref.at[pl.ds(owner * self.w, self.w), pl.ds(u * span, span), :]
            row = pl.multiple_of(u * span + owner * self.piece, self.piece)
            return ref.at[pl.ds(self.p[0] * self.w, self.w), pl.ds(row, self.piece), :]

        def slot(self, axis, u, d, s):
            if axis == 0:
                return rb1.at[u, d, pl.ds(s * self.w, self.w)]
            return rb2.at[u, d, pl.ds(0, self.w), pl.ds(s * self.piece, self.piece)]

        def name(self, axis, k):
            return lax.rem(self.p[axis] + k + self.n[axis], self.n[axis])

        def reduce_copy(self, axis, u, d, s):
            sign = 1 if d == 0 else -1
            h = self.hops(axis, u, d)
            if s == 0:
                src = self.chunk(acc, axis, u, self.name(axis, sign * h))
            else:
                src = self.slot(axis, u, d, s - 1)
            return pltpu.make_async_remote_copy(
                src_ref=src, dst_ref=self.slot(axis, u, d, s),
                send_sem=ring_ssem.at[axis, u, d, s], recv_sem=ring_rsem.at[axis, u, d, s],
                device_id=self.at[axis](sign), device_id_type=MESH,
            )

        def reduce_step(self, axis, u, d, s):
            if s >= self.hops(axis, u, d):
                return
            if s > 0:
                sign = 1 if d == 0 else -1
                h = self.hops(axis, u, d)
                self.reduce_copy(axis, u, d, s - 1).wait_recv()
                here = self.slot(axis, u, d, s - 1)
                here[...] += self.chunk(acc, axis, u, self.name(axis, sign * (h - s)))[...]
            self.reduce_copy(axis, u, d, s).start()

        def reduce_end(self, axis, u):
            value = self.chunk(acc, axis, u, self.p[axis])[...]
            for d in (1, 0) if u % 2 == 0 else (0, 1):
                h = self.hops(axis, u, d)
                if h:
                    self.reduce_copy(axis, u, d, h - 1).wait_recv()
                    value = value + self.slot(axis, u, d, h - 1)[...]
            target = acc if axis == 0 else full
            self.chunk(target, axis, u, self.p[axis])[...] = value

        def gather_copy(self, axis, u, d, s, back):
            sign = 1 if d == 0 else -1
            there = self.chunk(full, axis, u, self.name(axis, -sign * (s + back)))
            return pltpu.make_async_remote_copy(
                src_ref=there, dst_ref=there,
                send_sem=ring_ssem.at[2 + axis, u, d, s],
                recv_sem=ring_rsem.at[2 + axis, u, d, s],
                device_id=self.at[axis](sign), device_id_type=MESH,
            )

        def gather_step(self, axis, u, d, s):
            if s >= self.hops(axis, u, d):
                return
            if s > 0:
                self.gather_copy(axis, u, d, s - 1, 1).wait_recv()
            self.gather_copy(axis, u, d, s, 0).start()

        def gather_end(self, axis, u):
            for d in (0, 1):
                h = self.hops(axis, u, d)
                if h:
                    self.gather_copy(axis, u, d, h - 1, 1).wait_recv()

        def flows(self, axis):
            pairs = [(u, d) for u in range(SLICES) for d in (0, 1)]
            return sorted(pairs, key=lambda f: -self.hops(axis, *f))

        def longest(self, axis):
            return self.n[axis] // 2

        def start_long(self):
            for u, d in self.flows(0):
                if self.hops(0, u, d) == self.longest(0):
                    self.reduce_step(0, u, d, 0)

        def start_short(self):
            for u, d in self.flows(0):
                if self.hops(0, u, d) < self.longest(0):
                    self.reduce_step(0, u, d, 0)

        def middle(self):
            for s in range(1, self.longest(0)):
                for u, d in self.flows(0):
                    self.reduce_step(0, u, d, s)
            for u in range(SLICES):
                self.reduce_end(0, u)
                for d in (0, 1):
                    self.reduce_step(1, u, d, 0)
            for s in range(1, self.longest(1)):
                for u, d in self.flows(1):
                    self.reduce_step(1, u, d, s)
            for u in range(SLICES):
                self.reduce_end(1, u)
                for d in (0, 1):
                    self.gather_step(1, u, d, 0)
            for s in range(1, self.longest(1)):
                for u, d in self.flows(1):
                    self.gather_step(1, u, d, s)
            for u in range(SLICES):
                self.gather_end(1, u)
                for d in (0, 1):
                    self.gather_step(0, u, d, 0)
            for s in range(1, self.longest(0)):
                for u, d in self.flows(0):
                    self.gather_step(0, u, d, s)

        def drain(self):
            for axis in (0, 1):
                for u, d in self.flows(axis):
                    for s in range(self.hops(axis, u, d)):
                        self.reduce_copy(axis, u, d, s).wait_send()
                        self.gather_copy(axis, u, d, s, 0).wait_send()

    plans = (Plan(nz, ny, z, y, z_at, y_at), Plan(ny, nz, y, z, y_at, z_at))

    def each(act):
        for which in (0, 1):
            @pl.when(core == which)
            def _():
                act(plans[which])

    own_tile(0)
    each(lambda plan: plan.start_long())
    own_tile(1)
    own_tile(2)
    each(lambda plan: plan.start_short())
    own_tile(3)
    each(lambda plan: plan.middle())

    chip = z * ny + y
    home = chip * LANES // width
    place = lax.rem(chip, width // LANES)
    chip_rows = LANES

    def lhs_copy(u, k):
        return pltpu.make_async_remote_copy(
            src_ref=full.at[place, pl.ds(u * span, span), :],
            dst_ref=lhs.at[pl.ds(u * span, span), :],
            send_sem=lhs_ssem.at[u, k - 1], recv_sem=lhs_rsem.at[u],
            device_id=x_at(k), device_id_type=MESH,
        )

    for u in range(SLICES):
        each(lambda plan: plan.gather_end(0, u))

        @pl.when(x == home)
        def _():
            for k in range(1, nx):
                lhs_copy(u, k).start()
            lhs[pl.ds(u * span, span), :] = full[place, pl.ds(u * span, span), :]

    for u in range(SLICES):
        @pl.when(x != home)
        def _():
            lhs_copy(u, 1).wait_recv()

        left = lhs[pl.ds(u * span, span), :].T
        for t in range(tiles):
            right = jnp.concatenate(
                [full[t * per_tile + q, pl.ds(u * span, span), :] for q in range(per_tile)], axis=1
            )
            term = jnp.dot(
                left, right, precision=lax.Precision.HIGHEST, preferred_element_type=jnp.float32
            )
            cols = pl.ds(t * tile_w, tile_w)
            if u == 0:
                part[:, cols] = term
            else:
                part[:, cols] += term

    keep = chip_rows // 2
    trade = pltpu.make_async_remote_copy(
        src_ref=part.at[pl.ds(pl.multiple_of((1 - core) * keep, keep), keep), :],
        dst_ref=part_in,
        send_sem=part_ssem, recv_sem=part_rsem,
        device_id=partner, device_id_type=MESH,
    )
    trade.start()
    for k in range(1, nx):
        lin_copy(k).wait_send()
    for i in range(tiles):
        swap(i, theirs(i)).wait_send()
    each(lambda plan: plan.drain())

    @pl.when(x == home)
    def _():
        for u in range(SLICES):
            for k in range(1, nx):
                lhs_copy(u, k).wait_send()

    trade.wait_recv()
    count = rows * nz * ny * 2
    scale = jnp.float32(1.0) / jnp.float32(count)
    own = part[pl.ds(pl.multiple_of(core * keep, keep), keep), :]
    out_ref[...] = (own + part_in[...]) * scale
    trade.wait_send()


def per_device(clusters, ny, features, coef, log_exposure, claims, cluster_id, period, period_effect):
    rows, width = features.shape
    nx = lax.axis_size("gr")
    nz = lax.axis_size("cal") // (2 * ny)
    half = clusters // 2
    span = half // SLICES
    nchunk = width // LANES
    tiles = 4
    tile_w = width // tiles
    f32 = jnp.float32
    dma = pltpu.SemaphoreType.DMA
    depth = max(nchunk // 2, 1)
    vm = pl.BlockSpec(memory_space=pltpu.VMEM)
    return pl.pallas_call(
        functools.partial(meat_kernel, nz, ny, nx),
        out_shape=jax.ShapeDtypeStruct((LANES // 2, width), f32),
        in_specs=[pl.BlockSpec(memory_space=pl.ANY)] + [vm] * 6,
        out_specs=vm,
        scratch_shapes=[
            pltpu.VMEM((tiles, rows, tile_w), jnp.bfloat16),
            pltpu.VMEM((nx, 1, rows), f32),
            pltpu.VMEM((clusters, rows), jnp.bfloat16),
            pltpu.VMEM((nchunk, half, LANES), f32),
            pltpu.VMEM((nchunk, half, LANES), f32),
            pltpu.VMEM((nchunk, half, LANES), f32),
            pltpu.VMEM((SLICES, 2, depth, span, LANES), f32),
            pltpu.VMEM((SLICES, 2, 2, span // 2, LANES), f32),
            pltpu.VMEM((nchunk, half, LANES), f32),
            pltpu.VMEM((half, LANES), f32),
            pltpu.VMEM((LANES, width), f32),
            pltpu.VMEM((LANES // 2, width), f32),
            dma((tiles,)),
            dma((nx - 1,)),
            dma((nx - 1,)),
            dma((tiles,)),
            dma((tiles,)),
            dma((4, SLICES, 2, 4)),
            dma((4, SLICES, 2, 4)),
            dma((SLICES, nx - 1)),
            dma((SLICES,)),
            dma,
            dma,
        ],
        compiler_params=pltpu.CompilerParams(
            collective_id=0, has_side_effects=True, vmem_limit_bytes=60 * 1024 * 1024
        ),
    )(
        features,
        coef.reshape(1, width),
        log_exposure.reshape(1, rows),
        claims.reshape(1, rows),
        cluster_id.reshape(1, rows),
        period.reshape(1, rows),
        period_effect.reshape(1, -1),
    )


def solution(mesh, clusters=1024, ny=NY):
    placed = (P("cal", "gr"), P("gr"), P("cal"), P("cal"), P("cal"), P("cal"), P())
    return jax.shard_map(
        functools.partial(per_device, clusters, ny),
        mesh=mesh, in_specs=placed, out_specs=P("cal", "gr"), check_vma=False,
    )
```
